32 devices in a mesh: pipe: 4 (over z), dp: 2 (over x), tensor: 4 (over y, core).
Axes of the slice: x: 2, y: 2, z: 4, core: 2. Of those that a mesh axis runs over, the one named last changes fastest.
Arguments:
- acts: bfloat16 [4, 4, 128, 8192], P('pipe', None, 'dp', 'tensor'), may hold values from -6 to 6
- w_in: bfloat16 [4, 8192, 512], P('pipe', 'tensor', 'dp'), may hold values from -0.0625 to 0.0625
- w_out: bfloat16 [4, 512, 8192], P('pipe', 'dp', 'tensor'), may hold values from -0.25 to 0.25
- top_grad: bfloat16 [4, 128, 8192], P(None, 'dp', 'tensor'), may hold values from -6 to 6
Outputs:
- grad_input: bfloat16 [4, 4, 128, 8192], P('pipe', None, 'dp', 'tensor')
- grad_w_in: bfloat16 [4, 8192, 512], P('pipe', 'tensor', 'dp')
- grad_w_out: bfloat16 [4, 512, 8192], P('pipe', 'dp', 'tensor')
The draws below stay inside these ranges and needn't reach their ends.
All inputs are finite; a program needn't handle non-finite values.
Results may differ from the reference program's by a relative error of at most 0.013.
Values may be sent and summed in bfloat16 or wider, within the bound.
A program may use at most 64 MiB of HBM per device.

```python
import jax
import jax.numpy as jnp
from jax import lax

D = 8192
R = 512
M = 4
TOKM = 64
TOKENS = 128
SECTIONS = 4
N_PIPE = 4
N_DP = 2


def levels(rng, dims, cuts, least, top_value):
    loudness = 1.0
    for axis_at, parts in cuts:
        heights = jax.random.uniform(jax.random.fold_in(jax.random.fold_in(rng, 6), axis_at), (parts,), jnp.float32, least / len(cuts), top_value / len(cuts))
        loudness = loudness * jnp.repeat(jnp.exp(heights), dims[axis_at] // parts).reshape((-1,) + (1,) * (len(dims) - 1 - axis_at))
    return loudness


def bell_draw(stream_key, extent, scale, most, pieces=(), held_as=jnp.bfloat16):
    drawn = scale * jax.random.normal(stream_key, extent, jnp.float32)
    if pieces:
        drawn = drawn * levels(stream_key, extent, pieces, -0.22, 0.18)
    return jnp.clip(drawn, -most, most).astype(held_as)


def setup_inputs(seed: int = 0) -> dict:
    key_of = jax.random.split(jax.random.key(seed), 5)
    return {
        "acts": bell_draw(key_of[0], (SECTIONS, M, TOKENS, D), 1.0, 6.0, ((0, 4), (2, 2), (3, 4))),
        "w_in": bell_draw(key_of[1], (SECTIONS, D, R), D ** -0.5, 0.0625, ((0, 4), (1, 4), (2, 2))),
        "w_out": bell_draw(key_of[2], (SECTIONS, R, D), R ** -0.5, 0.25, ((0, 4), (1, 2), (2, 4))),
        "top_grad": bell_draw(key_of[3], (M, TOKENS, D), 1.0, 6.0, ((1, 2), (2, 4))),
    }


def silu_slope(value):
    sig = jax.nn.sigmoid(value)
    return sig * (1.0 + value * (1.0 - sig))


def block_sum(left, right):
    left4 = left.reshape(M, N_DP, TOKM, left.shape[-1])
    right4 = right.reshape(M, N_DP, TOKM, right.shape[-1])

    def step_fn(total, index):
        left_b = lax.dynamic_index_in_dim(left4, index, 1, keepdims=False).reshape(M * TOKM, -1)
        right_b = lax.dynamic_index_in_dim(right4, index, 1, keepdims=False).reshape(M * TOKM, -1)
        part = jnp.dot(left_b.T, right_b, preferred_element_type=jnp.float32)
        part = part.astype(jnp.bfloat16).astype(jnp.float32)
        return total + part, 0

    start = jnp.zeros((left.shape[-1], right.shape[-1]), jnp.float32)
    total, unused = lax.scan(step_fn, start, jnp.arange(N_DP, dtype=jnp.int32))
    return total.astype(jnp.bfloat16)


def reference(acts, w_in, w_out, top_grad):
    grad_now = top_grad.reshape(M * TOKENS, D)
    inputs_list = []
    w_in_list = []
    w_out_list = []
    for section in reversed(range(N_PIPE)):
        x_rows = acts[section].reshape(M * TOKENS, D).astype(jnp.float32)
        wi = w_in[section].astype(jnp.float32)
        wo = w_out[section].astype(jnp.float32)
        pre = jnp.dot(x_rows, wi, preferred_element_type=jnp.float32)
        act = jax.nn.silu(pre).astype(jnp.bfloat16)
        grad_f = grad_now.astype(jnp.float32)
        hidden = jnp.dot(grad_f, wo.T, preferred_element_type=jnp.float32)
        dpre = (hidden * silu_slope(pre)).astype(jnp.bfloat16)
        back = (grad_f + jnp.dot(dpre.astype(jnp.float32), wi.T, preferred_element_type=jnp.float32)).astype(jnp.bfloat16)
        w_in_list.append(block_sum(x_rows, dpre.astype(jnp.float32)))
        w_out_list.append(block_sum(act.astype(jnp.float32), grad_f))
        inputs_list.append(back.reshape(M, TOKENS, D))
        grad_now = back
    return jnp.stack(inputs_list[::-1]), jnp.stack(w_in_list[::-1]), jnp.stack(w_out_list[::-1])
```

```python
import functools

import jax
import jax.numpy as jnp
from jax import lax
from jax.experimental import pallas as pl
from jax.experimental.pallas import tpu as pltpu
from jax.sharding import PartitionSpec as P

MESH = pl.DeviceIdType.MESH
LAST = (((1,), (1,)), ((), ()))
FIRST = (((0,), (0,)), ((), ()))


def silu_slope(value):
    sig = jax.nn.sigmoid(value)
    return sig * (1.0 + value * (1.0 - sig))


def dot(left, right, dims):
    return lax.dot_general(left, right, dims, preferred_element_type=jnp.float32)


def chain(
    pipes, parts, chunks,
    x_ref, wi_ref, wo_ref, top_ref,
    back_ref, pin_ref, pout_ref,
    g_buf, pre_send, pre_recv, act_buf, hid_send, hid_recv, dpre_buf, slope_buf,
    pre_ss, pre_rs, act_ss, act_rs, hid_ss, hid_rs, dp_ss, dp_rs, g_ss, g_rs,
):
    micro, rows, width = x_ref.shape
    inner = wi_ref.shape[1]
    quarter = inner // parts
    step_w = width // chunks
    section = lax.axis_index("pipe")
    me = lax.axis_index("tensor")
    first = section == pipes - 1
    below = jnp.maximum(section - 1, 0)
    above = jnp.minimum(section + 1, pipes - 1)
    peers = [lax.rem(me + d, parts) for d in range(1, parts)]

    barrier = pltpu.get_barrier_semaphore()
    for peer in peers:
        pl.semaphore_signal(barrier, inc=1, device_id={"tensor": peer}, device_id_type=MESH)

    @pl.when(section > 0)
    def _():
        pl.semaphore_signal(barrier, inc=1, device_id={"pipe": below}, device_id_type=MESH)

    @pl.when(section < pipes - 1)
    def _():
        pl.semaphore_signal(barrier, inc=1, device_id={"pipe": above}, device_id_type=MESH)

    beside = jnp.minimum(section, 1) + jnp.minimum(pipes - 1 - section, 1)
    pl.semaphore_wait(barrier, parts - 1 + beside)

    def remote(src, dst, send, recv, where):
        return pltpu.make_async_remote_copy(
            src_ref=src, dst_ref=dst, send_sem=send, recv_sem=recv,
            device_id=where, device_id_type=MESH,
        )

    @pl.when(first)
    def _():
        g_buf[...] = top_ref[...]

    flat_x = x_ref[...].reshape(micro * rows, width)
    pre = jnp.dot(flat_x, wi_ref[...], preferred_element_type=jnp.float32)
    for t in range(parts):
        pre_send[t] = pre[:, t * quarter : (t + 1) * quarter]
    pre_copies = [
        remote(pre_send.at[peer], pre_recv.at[d], pre_ss.at[d], pre_rs.at[d], {"tensor": peer})
        for d, peer in enumerate(peers)
    ]
    for copy in pre_copies:
        copy.start()

    hid_copies = [
        [
            remote(hid_send.at[m, peer], hid_recv.at[m, d], hid_ss.at[m, d], hid_rs.at[m, d], {"tensor": peer})
            for d, peer in enumerate(peers)
        ]
        for m in range(micro)
    ]
    dp_copies = [
        [
            remote(dpre_buf.at[m, me], dpre_buf.at[m, me], dp_ss.at[m, d], dp_rs.at[m, d], {"tensor": peer})
            for d, peer in enumerate(peers)
        ]
        for m in range(micro)
    ]
    act_copies = [
        remote(act_buf.at[me], act_buf.at[me], act_ss.at[d], act_rs.at[d], {"tensor": peer})
        for d, peer in enumerate(peers)
    ]
    g_copies = [
        [
            remote(
                back_ref.at[m, :, pl.ds(c * step_w, step_w)], g_buf.at[m, :, pl.ds(c * step_w, step_w)],
                g_ss.at[m, c], g_rs.at[m, c], {"pipe": below},
            )
            for c in range(chunks)
        ]
        for m in range(micro)
    ]

    def hidden_start(m):
        @pl.when(section < pipes - 1)
        def _():
            for copy in g_copies[m]:
                copy.wait_recv()

        part = dot(g_buf[m], wo_ref[...], LAST)
        for t in range(parts):
            hid_send[m, t] = part[:, t * quarter : (t + 1) * quarter]
        for copy in hid_copies[m]:
            copy.start()

    hidden_start(0)
    for copy in pre_copies:
        copy.wait_recv()
    mine = pre_send[me]
    for d in range(parts - 1):
        mine = mine + pre_recv[d]
    slope_buf[...] = silu_slope(mine)
    act_buf[me] = jax.nn.silu(mine).astype(jnp.bfloat16)
    for copy in act_copies:
        copy.start()

    for m in range(micro):
        if m > 0:
            hidden_start(m)
        for copy in hid_copies[m]:
            copy.wait_recv()
        hidden = hid_send[m, me]
        for d in range(parts - 1):
            hidden = hidden + hid_recv[m, d]
        dpre_buf[m, me] = (hidden * slope_buf[m * rows : (m + 1) * rows, :]).astype(jnp.bfloat16)
        for copy in dp_copies[m]:
            copy.start()
        for copy in dp_copies[m]:
            copy.wait_recv()
        dpre = jnp.concatenate([dpre_buf[m, t] for t in range(parts)], axis=1)
        for c in range(chunks):
            cols = pl.ds(c * step_w, step_w)
            branch = dot(dpre, wi_ref[cols, :], LAST)
            back_ref[m, :, cols] = (g_buf[m, :, cols].astype(jnp.float32) + branch).astype(jnp.bfloat16)

            @pl.when(section > 0)
            def _():
                g_copies[m][c].start()

    for copy in act_copies:
        copy.wait_recv()
    act = jnp.concatenate([act_buf[t] for t in range(parts)], axis=1)
    dpre = jnp.concatenate(
        [dpre_buf[:, t].reshape(micro * rows, quarter) for t in range(parts)], axis=1
    )

    def grads(c, carry):
        cols = pl.ds(pl.multiple_of(c * step_w, step_w), step_w)
        x_cols = x_ref[:, :, cols].reshape(micro * rows, step_w)
        g_cols = g_buf[:, :, cols].reshape(micro * rows, step_w)
        pin_ref[cols, :] = dot(x_cols, dpre, FIRST).astype(jnp.bfloat16)
        pout_ref[:, cols] = dot(act, g_cols, FIRST).astype(jnp.bfloat16)
        return carry

    lax.fori_loop(0, chunks, grads, 0)

    for copy in pre_copies + act_copies:
        copy.wait_send()
    for m in range(micro):
        for copy in hid_copies[m] + dp_copies[m]:
            copy.wait_send()

        @pl.when(section > 0)
        def _():
            for copy in g_copies[m]:
                copy.wait_send()


def shards(acts, w_in, w_out, top_grad):
    pipes = lax.axis_size("pipe")
    parts = lax.axis_size("tensor")
    saved = acts[0]
    micro, rows, width = saved.shape
    w_in_full = lax.all_gather(w_in[0], "dp", axis=1, tiled=True)
    w_out_full = lax.all_gather(w_out[0], "dp", axis=0, tiled=True)
    inner = w_in_full.shape[1]
    quarter = inner // parts
    chunks = 4
    others = parts - 1
    bf, f32 = jnp.bfloat16, jnp.float32
    dma = pltpu.SemaphoreType.DMA
    vmem = pl.BlockSpec(memory_space=pltpu.VMEM)
    back, part_in, part_out = pl.pallas_call(
        functools.partial(chain, pipes, parts, chunks),
        out_shape=(
            jax.ShapeDtypeStruct((micro, rows, width), bf),
            jax.ShapeDtypeStruct((width, inner), bf),
            jax.ShapeDtypeStruct((inner, width), bf),
        ),
        in_specs=[vmem] * 4,
        out_specs=(vmem,) * 3,
        scratch_shapes=[
            pltpu.VMEM((micro, rows, width), bf),
            pltpu.VMEM((parts, micro * rows, quarter), f32),
            pltpu.VMEM((others, micro * rows, quarter), f32),
            pltpu.VMEM((parts, micro * rows, quarter), bf),
            pltpu.VMEM((micro, parts, rows, quarter), f32),
            pltpu.VMEM((micro, others, rows, quarter), f32),
            pltpu.VMEM((micro, parts, rows, quarter), bf),
            pltpu.VMEM((micro * rows, quarter), f32),
            dma((others,)), dma((others,)), dma((others,)), dma((others,)),
            dma((micro, others)), dma((micro, others)),
            dma((micro, others)), dma((micro, others)),
            dma((micro, chunks)), dma((micro, chunks)),
        ],
        compiler_params=pltpu.CompilerParams(
            collective_id=0, has_side_effects=True, vmem_limit_bytes=48 * 1024 * 1024
        ),
    )(saved, w_in_full, w_out_full, top_grad)
    grad_in = lax.psum_scatter(part_in, "dp", scatter_dimension=1, tiled=True)
    grad_out = lax.psum_scatter(part_out, "dp", scatter_dimension=0, tiled=True)
    return back[None], grad_in[None], grad_out[None]


def solution(mesh):
    placed = (
        P("pipe", None, "dp", "tensor"),
        P("pipe", "tensor", "dp"),
        P("pipe", "dp", "tensor"),
        P(None, "dp", "tensor"),
    )
    return jax.shard_map(
        shards,
        mesh=mesh,
        in_specs=placed,
        out_specs=(
            P("pipe", None, "dp", "tensor"),
            P("pipe", "tensor", "dp"),
            P("pipe", "dp", "tensor"),
        ),
        check_vma=False,
    )
```

```python
import functools

import jax
import jax.numpy as jnp
from jax import lax
from jax.experimental import pallas as pl
from jax.experimental.pallas import tpu as pltpu
from jax.sharding import PartitionSpec as P

MESH = pl.DeviceIdType.MESH
LAST = (((1,), (1,)), ((), ()))
FIRST = (((0,), (0,)), ((), ()))


def silu_slope(value):
    sig = jax.nn.sigmoid(value)
    return sig * (1.0 + value * (1.0 - sig))


def dot(left, right, dims):
    return lax.dot_general(left, right, dims, preferred_element_type=jnp.float32)


def chain(
    pipes, parts, pair, chunks,
    x_ref, wi_ref, wo_ref, top_ref,
    back_ref, pin_ref, pout_ref,
    g_buf, pre_send, pre_recv, act_buf, hid_send, hid_recv, dpre_buf, slope_buf,
    pre_ss, pre_rs, act_ss, act_rs, hid_ss, hid_rs, dp_ss, dp_rs, g_ss, g_rs,
    *across,
):
    micro, rows, width = x_ref.shape
    own = wi_ref.shape[1]
    halves = 2 if pair else 1
    per = parts // halves
    quarter = own // per
    step_w = width // chunks
    section = lax.axis_index("pipe")
    me = lax.axis_index("tensor")
    first = section == pipes - 1
    below = jnp.maximum(section - 1, 0)
    above = jnp.minimum(section + 1, pipes - 1)
    peers = [lax.rem(me + d, parts) for d in range(1, parts)]

    barrier = pltpu.get_barrier_semaphore()
    for peer in peers:
        pl.semaphore_signal(barrier, inc=1, device_id={"tensor": peer}, device_id_type=MESH)
    if pair:
        partner = {"dp": 1 - lax.axis_index("dp")}
        pl.semaphore_signal(barrier, inc=1, device_id=partner, device_id_type=MESH)

    @pl.when(section > 0)
    def _():
        pl.semaphore_signal(barrier, inc=1, device_id={"pipe": below}, device_id_type=MESH)

    @pl.when(section < pipes - 1)
    def _():
        pl.semaphore_signal(barrier, inc=1, device_id={"pipe": above}, device_id_type=MESH)

    beside = jnp.minimum(section, 1) + jnp.minimum(pipes - 1 - section, 1)
    pl.semaphore_wait(barrier, parts - 1 + halves - 1 + beside)

    def remote(src, dst, send, recv, where):
        return pltpu.make_async_remote_copy(
            src_ref=src, dst_ref=dst, send_sem=send, recv_sem=recv,
            device_id=where, device_id_type=MESH,
        )

    wi_halves, wo_halves = [wi_ref], [wo_ref]
    if pair:
        wi_other, wo_other, x_other, g_other, dpre_other, act_other, one_ss, one_rs, gx_ss, gx_rs, dx_ss, dx_rs = across
        wi_halves.append(wi_other)
        wo_halves.append(wo_other)
        wi_copy = remote(wi_ref, wi_other, one_ss.at[0], one_rs.at[0], partner)
        wo_copy = remote(wo_ref, wo_other, one_ss.at[1], one_rs.at[1], partner)
        x_copy = remote(x_ref, x_other, one_ss.at[2], one_rs.at[2], partner)
        actx_copy = remote(act_buf.at[pl.ds(per, per)], act_other, one_ss.at[3], one_rs.at[3], partner)
        gx_copies = [remote(g_buf.at[m], g_other.at[m], gx_ss.at[m], gx_rs.at[m], partner) for m in range(micro)]
        dx_copies = [
            remote(dpre_buf.at[m, pl.ds(per, per)], dpre_other.at[m], dx_ss.at[m], dx_rs.at[m], partner)
            for m in range(micro)
        ]
        wi_copy.start()

    @pl.when(first)
    def _():
        g_buf[...] = top_ref[...]

    pre_copies = [
        remote(pre_send.at[peer], pre_recv.at[d], pre_ss.at[d], pre_rs.at[d], {"tensor": peer})
        for d, peer in enumerate(peers)
    ]
    hid_copies = [
        [
            remote(hid_send.at[m, peer], hid_recv.at[m, d], hid_ss.at[m, d], hid_rs.at[m, d], {"tensor": peer})
            for d, peer in enumerate(peers)
        ]
        for m in range(micro)
    ]
    dp_copies = [
        [
            remote(dpre_buf.at[m, me], dpre_buf.at[m, me], dp_ss.at[m, d], dp_rs.at[m, d], {"tensor": peer})
            for d, peer in enumerate(peers)
        ]
        for m in range(micro)
    ]
    act_copies = [
        remote(act_buf.at[me], act_buf.at[me], act_ss.at[d], act_rs.at[d], {"tensor": peer})
        for d, peer in enumerate(peers)
    ]
    g_copies = [
        [
            remote(
                back_ref.at[m, :, pl.ds(c * step_w, step_w)], g_buf.at[m, :, pl.ds(c * step_w, step_w)],
                g_ss.at[m, c], g_rs.at[m, c], {"pipe": below},
            )
            for c in range(chunks)
        ]
        for m in range(micro)
    ]

    flat_x = x_ref[...].reshape(micro * rows, width)
    for h in range(halves):
        if h == 1:
            wi_copy.wait_recv()
            wo_copy.start()
        pre = jnp.dot(flat_x, wi_halves[h][...], preferred_element_type=jnp.float32)
        for t in range(per):
            pre_send[h * per + t] = pre[:, t * quarter : (t + 1) * quarter]
    for copy in pre_copies:
        copy.start()

    def hidden_now(which):
        count = len(which)
        g_now = g_buf[which[0] : which[-1] + 1].reshape(count * rows, width)
        for h in range(halves):
            part = dot(g_now, wo_halves[h][...], LAST)
            for t in range(per):
                for i, m in enumerate(which):
                    hid_send[m, h * per + t] = part[i * rows : (i + 1) * rows, t * quarter : (t + 1) * quarter]
        for m in which:
            for copy in hid_copies[m]:
                copy.start()
        if pair:
            for m in which:
                gx_copies[m].start()

    def dpre_now(m):
        for copy in hid_copies[m]:
            copy.wait_recv()
        hidden = hid_send[m, me]
        for d in range(parts - 1):
            hidden = hidden + hid_recv[m, d]
        dpre_buf[m, me] = (hidden * slope_buf[m * rows : (m + 1) * rows, :]).astype(jnp.bfloat16)
        for copy in dp_copies[m]:
            copy.start()

    for copy in pre_copies:
        copy.wait_recv()
    mine = pre_send[me]
    for d in range(parts - 1):
        mine = mine + pre_recv[d]
    slope_buf[...] = silu_slope(mine)
    act_buf[me] = jax.nn.silu(mine).astype(jnp.bfloat16)
    for copy in act_copies:
        copy.start()

    if pair:
        wo_copy.wait_recv()
        x_copy.start()

    @pl.when(first)
    def _():
        hidden_now(list(range(micro)))
        for m in range(micro):
            dpre_now(m)

    for m in range(micro):
        @pl.when(section < pipes - 1)
        def _():
            for copy in g_copies[m]:
                copy.wait_recv()
            hidden_now([m])
            dpre_now(m)

        for copy in dp_copies[m]:
            copy.wait_recv()
        dpre_halves = [
            jnp.concatenate([dpre_buf[m, h * per + t] for t in range(per)], axis=1) for h in range(halves)
        ]
        for c in range(chunks):
            cols = pl.ds(c * step_w, step_w)
            total = g_buf[m, :, cols].astype(jnp.float32)
            for h in range(halves):
                total = total + dot(dpre_halves[h], wi_halves[h][cols, :], LAST)
            back_ref[m, :, cols] = total.astype(jnp.bfloat16)

            @pl.when(section > 0)
            def _():
                g_copies[m][c].start()

        if pair:
            dx_copies[m].start()
        if m == 0:
            for copy in act_copies:
                copy.wait_recv()
            if pair:
                actx_copy.start()

    sources = [(x_ref, g_buf, act_buf, dpre_buf)]
    if pair:
        x_copy.wait_recv()
        actx_copy.wait_recv()
        for m in range(micro):
            gx_copies[m].wait_recv()
            dx_copies[m].wait_recv()
        sources.append((x_other, g_other, act_other, dpre_other))
    ready = []
    for x_from, g_from, act_from, dpre_from in sources:
        act = jnp.concatenate([act_from[t] for t in range(per)], axis=1)
        dpre = jnp.concatenate(
            [dpre_from[:, t].reshape(micro * rows, quarter) for t in range(per)], axis=1
        )
        ready.append((x_from, g_from, act, dpre))

    for c in range(chunks):
        cols = pl.ds(c * step_w, step_w)
        grad_in, grad_out = 0.0, 0.0
        for x_from, g_from, act, dpre in ready:
            x_cols = x_from[:, :, cols].reshape(micro * rows, step_w)
            g_cols = g_from[:, :, cols].reshape(micro * rows, step_w)
            grad_in = grad_in + dot(x_cols, dpre, FIRST)
            grad_out = grad_out + dot(act, g_cols, FIRST)
        pin_ref[cols, :] = grad_in.astype(jnp.bfloat16)
        pout_ref[:, cols] = grad_out.astype(jnp.bfloat16)

    for copy in pre_copies + act_copies:
        copy.wait_send()
    if pair:
        for copy in [wi_copy, wo_copy, x_copy, actx_copy] + gx_copies + dx_copies:
            copy.wait_send()
    for m in range(micro):
        for copy in hid_copies[m] + dp_copies[m]:
            copy.wait_send()

        @pl.when(section > 0)
        def _():
            for copy in g_copies[m]:
                copy.wait_send()


def shards(acts, w_in, w_out, top_grad):
    pipes = lax.axis_size("pipe")
    parts = lax.axis_size("tensor")
    pair = lax.axis_size("dp") == 2 and parts % 2 == 0
    saved = acts[0]
    micro, rows, width = saved.shape
    if pair:
        w_in_now, w_out_now = w_in[0], w_out[0]
    else:
        w_in_now = lax.all_gather(w_in[0], "dp", axis=1, tiled=True)
        w_out_now = lax.all_gather(w_out[0], "dp", axis=0, tiled=True)
    own = w_in_now.shape[1]
    per = parts // 2 if pair else parts
    quarter = own // per
    chunks = 4
    others = parts - 1
    bf, f32 = jnp.bfloat16, jnp.float32
    dma = pltpu.SemaphoreType.DMA
    vmem = pl.BlockSpec(memory_space=pltpu.VMEM)
    across = []
    if pair:
        across = [
            pltpu.VMEM((width, own), bf),
            pltpu.VMEM((own, width), bf),
            pltpu.VMEM((micro, rows, width), bf),
            pltpu.VMEM((micro, rows, width), bf),
            pltpu.VMEM((micro, per, rows, quarter), bf),
            pltpu.VMEM((per, micro * rows, quarter), bf),
            dma((4,)), dma((4,)),
            dma((micro,)), dma((micro,)), dma((micro,)), dma((micro,)),
        ]
    back, grad_in, grad_out = pl.pallas_call(
        functools.partial(chain, pipes, parts, pair, chunks),
        out_shape=(
            jax.ShapeDtypeStruct((micro, rows, width), bf),
            jax.ShapeDtypeStruct((width, own), bf),
            jax.ShapeDtypeStruct((own, width), bf),
        ),
        in_specs=[vmem] * 4,
        out_specs=(vmem,) * 3,
        scratch_shapes=[
            pltpu.VMEM((micro, rows, width), bf),
            pltpu.VMEM((parts, micro * rows, quarter), f32),
            pltpu.VMEM((others, micro * rows, quarter), f32),
            pltpu.VMEM((parts, micro * rows, quarter), bf),
            pltpu.VMEM((micro, parts, rows, quarter), f32),
            pltpu.VMEM((micro, others, rows, quarter), f32),
            pltpu.VMEM((micro, parts, rows, quarter), bf),
            pltpu.VMEM((micro * rows, quarter), f32),
            dma((others,)), dma((others,)), dma((others,)), dma((others,)),
            dma((micro, others)), dma((micro, others)),
            dma((micro, others)), dma((micro, others)),
            dma((micro, chunks)), dma((micro, chunks)),
            *across,
        ],
        compiler_params=pltpu.CompilerParams(
            collective_id=0, has_side_effects=True, vmem_limit_bytes=48 * 1024 * 1024
        ),
    )(saved, w_in_now, w_out_now, top_grad)
    if not pair:
        grad_in = lax.psum_scatter(grad_in, "dp", scatter_dimension=1, tiled=True)
        grad_out = lax.psum_scatter(grad_out, "dp", scatter_dimension=0, tiled=True)
    return back[None], grad_in[None], grad_out[None]


def solution(mesh):
    placed = (
        P("pipe", None, "dp", "tensor"),
        P("pipe", "tensor", "dp"),
        P("pipe", "dp", "tensor"),
        P(None, "dp", "tensor"),
    )
    return jax.shard_map(
        shards,
        mesh=mesh,
        in_specs=placed,
        out_specs=(
            P("pipe", None, "dp", "tensor"),
            P("pipe", "tensor", "dp"),
            P("pipe", "dp", "tensor"),
        ),
        check_vma=False,
    )
```

```python
import functools

import jax
import jax.numpy as jnp
from jax import lax
from jax.experimental import pallas as pl
from jax.experimental.pallas import tpu as pltpu
from jax.sharding import PartitionSpec as P

MESH = pl.DeviceIdType.MESH
LAST = (((1,), (1,)), ((), ()))
FIRST = (((0,), (0,)), ((), ()))


def silu_slope(value):
    sig = jax.nn.sigmoid(value)
    return sig * (1.0 + value * (1.0 - sig))


def dot(left, right, dims):
    return lax.dot_general(left, right, dims, preferred_element_type=jnp.float32)


def chain(
    pipes, parts, pair, chunks,
    x_ref, wi_ref, wo_ref, top_ref,
    back_ref, pin_ref, pout_ref,
    g_buf, pre_send, pre_recv, act_buf, hid_send, hid_recv, dpre_buf, slope_buf,
    pre_ss, pre_rs, act_ss, act_rs, hid_ss, hid_rs, dp_ss, dp_rs, g_ss, g_rs,
    *across,
):
    micro, rows, width = x_ref.shape
    own = wi_ref.shape[1]
    halves = 2 if pair else 1
    per = parts // halves
    quarter = own // per
    step_w = width // chunks
    section = lax.axis_index("pipe")
    me = lax.axis_index("tensor")
    first = section == pipes - 1
    below = jnp.maximum(section - 1, 0)
    above = jnp.minimum(section + 1, pipes - 1)
    peers = [lax.rem(me + d, parts) for d in range(1, parts)]

    barrier = pltpu.get_barrier_semaphore()
    for peer in peers:
        pl.semaphore_signal(barrier, inc=1, device_id={"tensor": peer}, device_id_type=MESH)
    if pair:
        other_dp = 1 - lax.axis_index("dp")
        partner = {"dp": other_dp}
        for t in range(parts):
            pl.semaphore_signal(barrier, inc=1, device_id={"dp": other_dp, "tensor": t}, device_id_type=MESH)

    @pl.when(section > 0)
    def _():
        pl.semaphore_signal(barrier, inc=1, device_id={"pipe": below}, device_id_type=MESH)

    @pl.when(section < pipes - 1)
    def _():
        pl.semaphore_signal(barrier, inc=1, device_id={"pipe": above}, device_id_type=MESH)

    beside = jnp.minimum(section, 1) + jnp.minimum(pipes - 1 - section, 1)
    pl.semaphore_wait(barrier, parts - 1 + (halves - 1) * parts + beside)

    def remote(src, dst, send, recv, where):
        return pltpu.make_async_remote_copy(
            src_ref=src, dst_ref=dst, send_sem=send, recv_sem=recv,
            device_id=where, device_id_type=MESH,
        )

    wi_halves, wo_halves = [wi_ref], [wo_ref]
    if pair:
        wi_other, wo_other, x_other, g_other, dpre_other, act_other, one_ss, one_rs, gx_ss, gx_rs, dx_ss, dx_rs, top_recv, top_ss, top_rs = across
        wi_halves.append(wi_other)
        wo_halves.append(wo_other)
        wi_copy = remote(wi_ref, wi_other, one_ss.at[0], one_rs.at[0], partner)
        wo_copy = remote(wo_ref, wo_other, one_ss.at[1], one_rs.at[1], partner)
        x_copy = remote(x_ref, x_other, one_ss.at[2], one_rs.at[2], partner)
        actx_copy = remote(act_buf.at[pl.ds(per, per)], act_other, one_ss.at[3], one_rs.at[3], partner)
        gx_copies = [remote(g_buf.at[m], g_other.at[m], gx_ss.at[m], gx_rs.at[m], partner) for m in range(micro)]
        dx_copies = [
            remote(dpre_buf.at[m, pl.ds(per, per)], dpre_other.at[m], dx_ss.at[m], dx_rs.at[m], partner)
            for m in range(micro)
        ]
        wi_copy.start()

    @pl.when(first)
    def _():
        g_buf[...] = top_ref[...]

    pre_copies = [
        remote(pre_send.at[peer], pre_recv.at[d], pre_ss.at[d], pre_rs.at[d], {"tensor": peer})
        for d, peer in enumerate(peers)
    ]
    hid_copies = [
        [
            remote(hid_send.at[m, peer], hid_recv.at[m, d], hid_ss.at[m, d], hid_rs.at[m, d], {"tensor": peer})
            for d, peer in enumerate(peers)
        ]
        for m in range(micro)
    ]
    dp_copies = [
        [
            remote(dpre_buf.at[m, me], dpre_buf.at[m, me], dp_ss.at[m, d], dp_rs.at[m, d], {"tensor": peer})
            for d, peer in enumerate(peers)
        ]
        for m in range(micro)
    ]
    act_copies = [
        remote(act_buf.at[me], act_buf.at[me], act_ss.at[d], act_rs.at[d], {"tensor": peer})
        for d, peer in enumerate(peers)
    ]
    g_copies = [
        [
            remote(
                back_ref.at[m, :, pl.ds(c * step_w, step_w)], g_buf.at[m, :, pl.ds(c * step_w, step_w)],
                g_ss.at[m, c], g_rs.at[m, c], {"pipe": below},
            )
            for c in range(chunks)
        ]
        for m in range(micro)
    ]

    flat_x = x_ref[...].reshape(micro * rows, width)
    for h in range(halves):
        if h == 1:
            wi_copy.wait_recv()

            @pl.when(first)
            def _():
                gx_copies[0].start()

            @pl.when(section < pipes - 1)
            def _():
                wo_copy.start()

        pre = jnp.dot(flat_x, wi_halves[h][...], preferred_element_type=jnp.float32)
        for t in range(per):
            pre_send[h * per + t] = pre[:, t * quarter : (t + 1) * quarter]
    for copy in pre_copies:
        copy.start()

    def top_copy(m, q):
        where = {"tensor": q} if q < per else {"dp": other_dp, "tensor": q}
        return remote(hid_send.at[m, q], top_recv.at[m, me], top_ss.at[m, q], top_rs.at[m, me], where)

    def top_wait(m, t):
        return remote(hid_send.at[m, t], top_recv.at[m, t], top_ss.at[m, t], top_rs.at[m, t], {"tensor": peers[0]})

    def hidden_top(m):
        gx_copies[m].wait_recv()
        if m + 1 < micro:
            gx_copies[m + 1].start()
        else:
            x_copy.start()
        part = dot(jnp.concatenate([g_buf[m], g_other[m]], axis=0), wo_ref[...], LAST)
        for q in range(parts):
            at = (q % per) * quarter
            low = 0 if q < per else rows
            hid_send[m, q] = part[low : low + rows, at : at + quarter]
            if q < per:
                @pl.when(me == q)
                def _():
                    top_recv[m, q] = part[low : low + rows, at : at + quarter]

                @pl.when(me != q)
                def _():
                    top_copy(m, q).start()
            else:
                top_copy(m, q).start()

    def hidden_chain(m):
        for h in range(halves):
            part = dot(g_buf[m], wo_halves[h][...], LAST)
            for t in range(per):
                hid_send[m, h * per + t] = part[:, t * quarter : (t + 1) * quarter]
        for copy in hid_copies[m]:
            copy.start()
        if pair:
            gx_copies[m].start()

    def hidden_now(m):
        @pl.when(first)
        def _():
            if pair:
                hidden_top(m)
            else:
                hidden_chain(m)

        @pl.when(section < pipes - 1)
        def _():
            for copy in g_copies[m]:
                copy.wait_recv()
            hidden_chain(m)

    def dpre_finish(m, hidden):
        dpre_buf[m, me] = (hidden * slope_buf[m * rows : (m + 1) * rows, :]).astype(jnp.bfloat16)
        for copy in dp_copies[m]:
            copy.start()

    def dpre_chain(m):
        for copy in hid_copies[m]:
            copy.wait_recv()
        hidden = hid_send[m, me]
        for d in range(parts - 1):
            hidden = hidden + hid_recv[m, d]
        dpre_finish(m, hidden)

    def dpre_top(m):
        for t in range(parts):
            if t < per:
                @pl.when(me != t)
                def _():
                    top_wait(m, t).wait_recv()
            else:
                top_wait(m, t).wait_recv()
        hidden = top_recv[m, 0]
        for t in range(1, parts):
            hidden = hidden + top_recv[m, t]
        dpre_finish(m, hidden)

    def dpre_now(m):
        if not pair:
            dpre_chain(m)
            return

        @pl.when(first)
        def _():
            dpre_top(m)

        @pl.when(section < pipes - 1)
        def _():
            dpre_chain(m)

    for copy in pre_copies:
        copy.wait_recv()
    mine = pre_send[me]
    for d in range(parts - 1):
        mine = mine + pre_recv[d]
    slope_buf[...] = silu_slope(mine)
    act_buf[me] = jax.nn.silu(mine).astype(jnp.bfloat16)
    for copy in act_copies:
        copy.start()

    if pair:
        @pl.when(section < pipes - 1)
        def _():
            wo_copy.wait_recv()
            x_copy.start()

    hidden_now(0)
    for m in range(micro):
        dpre_now(m)
        if m + 1 < micro:
            hidden_now(m + 1)
        for copy in dp_copies[m]:
            copy.wait_recv()
        dpre_halves = [
            jnp.concatenate([dpre_buf[m, h * per + t] for t in range(per)], axis=1) for h in range(halves)
        ]
        for c in range(chunks):
            cols = pl.ds(c * step_w, step_w)
            total = g_buf[m, :, cols].astype(jnp.float32)
            for h in range(halves):
                total = total + dot(dpre_halves[h], wi_halves[h][cols, :], LAST)
            back_ref[m, :, cols] = total.astype(jnp.bfloat16)

            @pl.when(section > 0)
            def _():
                g_copies[m][c].start()

        if pair:
            dx_copies[m].start()
        if m == 0:
            for copy in act_copies:
                copy.wait_recv()
            if pair:
                actx_copy.start()

    sources = [(x_ref, g_buf, act_buf, dpre_buf)]
    if pair:
        x_copy.wait_recv()
        actx_copy.wait_recv()
        for m in range(micro):
            @pl.when(section < pipes - 1)
            def _():
                gx_copies[m].wait_recv()

            dx_copies[m].wait_recv()
        sources.append((x_other, g_other, act_other, dpre_other))
    ready = []
    for x_from, g_from, act_from, dpre_from in sources:
        act = jnp.concatenate([act_from[t] for t in range(per)], axis=1)
        dpre = jnp.concatenate(
            [dpre_from[:, t].reshape(micro * rows, quarter) for t in range(per)], axis=1
        )
        ready.append((x_from, g_from, act, dpre))

    for c in range(chunks):
        cols = pl.ds(c * step_w, step_w)
        grad_in, grad_out = 0.0, 0.0
        for x_from, g_from, act, dpre in ready:
            x_cols = x_from[:, :, cols].reshape(micro * rows, step_w)
            g_cols = g_from[:, :, cols].reshape(micro * rows, step_w)
            grad_in = grad_in + dot(x_cols, dpre, FIRST)
            grad_out = grad_out + dot(act, g_cols, FIRST)
        pin_ref[cols, :] = grad_in.astype(jnp.bfloat16)
        pout_ref[:, cols] = grad_out.astype(jnp.bfloat16)

    for copy in pre_copies + act_copies:
        copy.wait_send()
    if pair:
        for copy in [wi_copy, x_copy, actx_copy] + gx_copies + dx_copies:
            copy.wait_send()

        @pl.when(first)
        def _():
            for m in range(micro):
                for q in range(parts):
                    if q < per:
                        @pl.when(me != q)
                        def _():
                            top_copy(m, q).wait_send()
                    else:
                        top_copy(m, q).wait_send()

        @pl.when(section < pipes - 1)
        def _():
            wo_copy.wait_send()
            for m in range(micro):
                for copy in hid_copies[m]:
                    copy.wait_send()
    else:
        for m in range(micro):
            for copy in hid_copies[m]:
                copy.wait_send()
    for m in range(micro):
        for copy in dp_copies[m]:
            copy.wait_send()

        @pl.when(section > 0)
        def _():
            for copy in g_copies[m]:
                copy.wait_send()


def shards(acts, w_in, w_out, top_grad):
    pipes = lax.axis_size("pipe")
    parts = lax.axis_size("tensor")
    pair = lax.axis_size("dp") == 2 and parts % 2 == 0
    saved = acts[0]
    micro, rows, width = saved.shape
    if pair:
        w_in_now, w_out_now = w_in[0], w_out[0]
    else:
        w_in_now = lax.all_gather(w_in[0], "dp", axis=1, tiled=True)
        w_out_now = lax.all_gather(w_out[0], "dp", axis=0, tiled=True)
    own = w_in_now.shape[1]
    per = parts // 2 if pair else parts
    quarter = own // per
    chunks = 4
    others = parts - 1
    bf, f32 = jnp.bfloat16, jnp.float32
    dma = pltpu.SemaphoreType.DMA
    vmem = pl.BlockSpec(memory_space=pltpu.VMEM)
    across = []
    if pair:
        across = [
            pltpu.VMEM((width, own), bf),
            pltpu.VMEM((own, width), bf),
            pltpu.VMEM((micro, rows, width), bf),
            pltpu.VMEM((micro, rows, width), bf),
            pltpu.VMEM((micro, per, rows, quarter), bf),
            pltpu.VMEM((per, micro * rows, quarter), bf),
            dma((4,)), dma((4,)),
            dma((micro,)), dma((micro,)), dma((micro,)), dma((micro,)),
            pltpu.VMEM((micro, parts, rows, quarter), f32),
            dma((micro, parts)), dma((micro, parts)),
        ]
    back, grad_in, grad_out = pl.pallas_call(
        functools.partial(chain, pipes, parts, pair, chunks),
        out_shape=(
            jax.ShapeDtypeStruct((micro, rows, width), bf),
            jax.ShapeDtypeStruct((width, own), bf),
            jax.ShapeDtypeStruct((own, width), bf),
        ),
        in_specs=[vmem] * 4,
        out_specs=(vmem,) * 3,
        scratch_shapes=[
            pltpu.VMEM((micro, rows, width), bf),
            pltpu.VMEM((parts, micro * rows, quarter), f32),
            pltpu.VMEM((others, micro * rows, quarter), f32),
            pltpu.VMEM((parts, micro * rows, quarter), bf),
            pltpu.VMEM((micro, parts, rows, quarter), f32),
            pltpu.VMEM((micro, others, rows, quarter), f32),
            pltpu.VMEM((micro, parts, rows, quarter), bf),
            pltpu.VMEM((micro * rows, quarter), f32),
            dma((others,)), dma((others,)), dma((others,)), dma((others,)),
            dma((micro, others)), dma((micro, others)),
            dma((micro, others)), dma((micro, others)),
            dma((micro, chunks)), dma((micro, chunks)),
            *across,
        ],
        compiler_params=pltpu.CompilerParams(
            collective_id=0, has_side_effects=True, vmem_limit_bytes=48 * 1024 * 1024
        ),
    )(saved, w_in_now, w_out_now, top_grad)
    if not pair:
        grad_in = lax.psum_scatter(grad_in, "dp", scatter_dimension=1, tiled=True)
        grad_out = lax.psum_scatter(grad_out, "dp", scatter_dimension=0, tiled=True)
    return back[None], grad_in[None], grad_out[None]


def solution(mesh):
    placed = (
        P("pipe", None, "dp", "tensor"),
        P("pipe", "tensor", "dp"),
        P("pipe", "dp", "tensor"),
        P(None, "dp", "tensor"),
    )
    return jax.shard_map(
        shards,
        mesh=mesh,
        in_specs=placed,
        out_specs=(
            P("pipe", None, "dp", "tensor"),
            P("pipe", "tensor", "dp"),
            P("pipe", "dp", "tensor"),
        ),
        check_vma=False,
    )
```

```python
import functools

import jax
import jax.numpy as jnp
from jax import lax
from jax.experimental import pallas as pl
from jax.experimental.pallas import tpu as pltpu
from jax.sharding import PartitionSpec as P

MESH = pl.DeviceIdType.MESH
LAST = (((1,), (1,)), ((), ()))
FIRST = (((0,), (0,)), ((), ()))


def silu_slope(value):
    sig = jax.nn.sigmoid(value)
    return sig * (1.0 + value * (1.0 - sig))


def dot(left, right, dims):
    return lax.dot_general(left, right, dims, preferred_element_type=jnp.float32)


def chain(
    pipes, parts, pair, chunks,
    x_ref, wi_ref, wo_ref, top_ref,
    back_ref, pin_ref, pout_ref,
    g_buf, pre_send, pre_recv, act_buf, hid_send, hid_recv, dpre_buf, slope_buf,
    pre_ss, pre_rs, act_ss, act_rs, hid_ss, hid_rs, dp_ss, dp_rs, g_ss, g_rs,
    *across,
):
    micro, rows, width = x_ref.shape
    own = wi_ref.shape[1]
    halves = 2 if pair else 1
    per = parts // halves
    quarter = own // per
    step_w = width // chunks
    section = lax.axis_index("pipe")
    me = lax.axis_index("tensor")
    first = section == pipes - 1
    below = jnp.maximum(section - 1, 0)
    above = jnp.minimum(section + 1, pipes - 1)
    peers = [lax.rem(me + d, parts) for d in range(1, parts)]

    barrier = pltpu.get_barrier_semaphore()
    for peer in peers:
        pl.semaphore_signal(barrier, inc=1, device_id={"tensor": peer}, device_id_type=MESH)
    if pair:
        other_dp = 1 - lax.axis_index("dp")
        partner = {"dp": other_dp}
        for t in range(parts):
            pl.semaphore_signal(barrier, inc=1, device_id={"dp": other_dp, "tensor": t}, device_id_type=MESH)

    @pl.when(section > 0)
    def _():
        pl.semaphore_signal(barrier, inc=1, device_id={"pipe": below}, device_id_type=MESH)

    @pl.when(section < pipes - 1)
    def _():
        pl.semaphore_signal(barrier, inc=1, device_id={"pipe": above}, device_id_type=MESH)

    beside = jnp.minimum(section, 1) + jnp.minimum(pipes - 1 - section, 1)
    pl.semaphore_wait(barrier, parts - 1 + (halves - 1) * parts + beside)

    def remote(src, dst, send, recv, where):
        return pltpu.make_async_remote_copy(
            src_ref=src, dst_ref=dst, send_sem=send, recv_sem=recv,
            device_id=where, device_id_type=MESH,
        )

    wi_halves, wo_halves = [wi_ref], [wo_ref]
    if pair:
        wi_other, wo_other, x_other, g_other, dpre_other, act_other, one_ss, one_rs, gx_ss, gx_rs, dx_ss, dx_rs, top_recv, top_ss, top_rs = across
        wi_halves.append(wi_other)
        wo_halves.append(wo_other)
        wi_copy = remote(wi_ref, wi_other, one_ss.at[0], one_rs.at[0], partner)
        wo_copy = remote(wo_ref, wo_other, one_ss.at[1], one_rs.at[1], partner)
        x_copy = remote(x_ref, x_other, one_ss.at[2], one_rs.at[2], partner)
        actx_copy = remote(act_buf.at[pl.ds(per, per)], act_other, one_ss.at[3], one_rs.at[3], partner)
        gx_copies = [remote(g_buf.at[m], g_other.at[m], gx_ss.at[m], gx_rs.at[m], partner) for m in range(micro)]
        dx_copies = [
            remote(dpre_buf.at[m, pl.ds(per, per)], dpre_other.at[m], dx_ss.at[m], dx_rs.at[m], partner)
            for m in range(micro)
        ]
        wi_copy.start()

    @pl.when(first)
    def _():
        g_buf[...] = top_ref[...]

    pre_copies = [
        remote(pre_send.at[peer], pre_recv.at[d], pre_ss.at[d], pre_rs.at[d], {"tensor": peer})
        for d, peer in enumerate(peers)
    ]
    hid_copies = [
        [
            remote(hid_send.at[m, peer], hid_recv.at[m, d], hid_ss.at[m, d], hid_rs.at[m, d], {"tensor": peer})
            for d, peer in enumerate(peers)
        ]
        for m in range(micro)
    ]
    dp_copies = [
        [
            remote(dpre_buf.at[m, me], dpre_buf.at[m, me], dp_ss.at[m, d], dp_rs.at[m, d], {"tensor": peer})
            for d, peer in enumerate(peers)
        ]
        for m in range(micro)
    ]
    act_copies = [
        remote(act_buf.at[me], act_buf.at[me], act_ss.at[d], act_rs.at[d], {"tensor": peer})
        for d, peer in enumerate(peers)
    ]
    g_copies = [
        [
            remote(
                back_ref.at[m, :, pl.ds(c * step_w, step_w)], g_buf.at[m, :, pl.ds(c * step_w, step_w)],
                g_ss.at[m, c], g_rs.at[m, c], {"pipe": below},
            )
            for c in range(chunks)
        ]
        for m in range(micro)
    ]

    flat_x = x_ref[...].reshape(micro * rows, width)
    for h in range(halves):
        if h == 1:
            wi_copy.wait_recv()

            @pl.when(first)
            def _():
                gx_copies[0].start()

            @pl.when(section < pipes - 1)
            def _():
                wo_copy.start()

        pre = jnp.dot(flat_x, wi_halves[h][...], preferred_element_type=jnp.float32)
        for t in range(per):
            pre_send[h * per + t] = pre[:, t * quarter : (t + 1) * quarter]
    for copy in pre_copies:
        copy.start()

    def top_copy(m, q):
        where = {"tensor": q} if q < per else {"dp": other_dp, "tensor": q}
        return remote(hid_send.at[m, q], top_recv.at[m, me], top_ss.at[m, q], top_rs.at[m, me], where)

    def top_wait(m, t):
        return remote(hid_send.at[m, t], top_recv.at[m, t], top_ss.at[m, t], top_rs.at[m, t], {"tensor": peers[0]})

    def hidden_top(m):
        gx_copies[m].wait_recv()
        if m + 1 < micro:
            gx_copies[m + 1].start()
        else:
            x_copy.start()
        part = dot(jnp.concatenate([g_buf[m], g_other[m]], axis=0), wo_ref[...], LAST)
        for q in range(parts):
            at = (q % per) * quarter
            low = 0 if q < per else rows
            hid_send[m, q] = part[low : low + rows, at : at + quarter]
            if q < per:
                @pl.when(me == q)
                def _():
                    top_recv[m, q] = part[low : low + rows, at : at + quarter]

                @pl.when(me != q)
                def _():
                    top_copy(m, q).start()
            else:
                top_copy(m, q).start()

    def hidden_chain(m):
        for h in range(halves):
            part = dot(g_buf[m], wo_halves[h][...], LAST)
            for t in range(per):
                hid_send[m, h * per + t] = part[:, t * quarter : (t + 1) * quarter]
        for copy in hid_copies[m]:
            copy.start()
        if pair:
            gx_copies[m].start()

    def hidden_now(m):
        @pl.when(first)
        def _():
            if pair:
                hidden_top(m)
            else:
                hidden_chain(m)

        @pl.when(section < pipes - 1)
        def _():
            for copy in g_copies[m]:
                copy.wait_recv()
            hidden_chain(m)

    def dpre_finish(m, hidden):
        dpre_buf[m, me] = (hidden * slope_buf[m * rows : (m + 1) * rows, :]).astype(jnp.bfloat16)
        for copy in dp_copies[m]:
            copy.start()

    def dpre_chain(m):
        for copy in hid_copies[m]:
            copy.wait_recv()
        hidden = hid_send[m, me]
        for d in range(parts - 1):
            hidden = hidden + hid_recv[m, d]
        dpre_finish(m, hidden)

    def dpre_top(m):
        for t in range(parts):
            if t < per:
                @pl.when(me != t)
                def _():
                    top_wait(m, t).wait_recv()
            else:
                top_wait(m, t).wait_recv()
        hidden = top_recv[m, 0]
        for t in range(1, parts):
            hidden = hidden + top_recv[m, t]
        dpre_finish(m, hidden)

    def dpre_now(m):
        if not pair:
            dpre_chain(m)
            return

        @pl.when(first)
        def _():
            dpre_top(m)

        @pl.when(section < pipes - 1)
        def _():
            dpre_chain(m)

    for copy in pre_copies:
        copy.wait_recv()
    mine = pre_send[me]
    for d in range(parts - 1):
        mine = mine + pre_recv[d]
    slope_buf[...] = silu_slope(mine)
    act_buf[me] = jax.nn.silu(mine).astype(jnp.bfloat16)
    for copy in act_copies:
        copy.start()

    if pair:
        @pl.when(section < pipes - 1)
        def _():
            wo_copy.wait_recv()
            x_copy.start()

    for m in range(micro):
        hidden_now(m)
        dpre_now(m)
        for copy in dp_copies[m]:
            copy.wait_recv()
        dpre_halves = [
            jnp.concatenate([dpre_buf[m, h * per + t] for t in range(per)], axis=1) for h in range(halves)
        ]
        for c in range(chunks):
            cols = pl.ds(c * step_w, step_w)
            total = g_buf[m, :, cols].astype(jnp.float32)
            for h in range(halves):
                total = total + dot(dpre_halves[h], wi_halves[h][cols, :], LAST)
            back_ref[m, :, cols] = total.astype(jnp.bfloat16)

            @pl.when(section > 0)
            def _():
                g_copies[m][c].start()

        if pair:
            dx_copies[m].start()
        if m == 0:
            for copy in act_copies:
                copy.wait_recv()
            if pair:
                actx_copy.start()

    sources = [(x_ref, g_buf, act_buf, dpre_buf)]
    if pair:
        x_copy.wait_recv()
        actx_copy.wait_recv()
        for m in range(micro):
            @pl.when(section < pipes - 1)
            def _():
                gx_copies[m].wait_recv()

            dx_copies[m].wait_recv()
        sources.append((x_other, g_other, act_other, dpre_other))
    ready = []
    for x_from, g_from, act_from, dpre_from in sources:
        act = jnp.concatenate([act_from[t] for t in range(per)], axis=1)
        dpre = jnp.concatenate(
            [dpre_from[:, t].reshape(micro * rows, quarter) for t in range(per)], axis=1
        )
        ready.append((x_from, g_from, act, dpre))

    for c in range(chunks):
        cols = pl.ds(c * step_w, step_w)
        grad_in, grad_out = 0.0, 0.0
        for x_from, g_from, act, dpre in ready:
            x_cols = x_from[:, :, cols].reshape(micro * rows, step_w)
            g_cols = g_from[:, :, cols].reshape(micro * rows, step_w)
            grad_in = grad_in + dot(x_cols, dpre, FIRST)
            grad_out = grad_out + dot(act, g_cols, FIRST)
        pin_ref[cols, :] = grad_in.astype(jnp.bfloat16)
        pout_ref[:, cols] = grad_out.astype(jnp.bfloat16)

    for copy in pre_copies + act_copies:
        copy.wait_send()
    if pair:
        for copy in [wi_copy, x_copy, actx_copy] + gx_copies + dx_copies:
            copy.wait_send()

        @pl.when(first)
        def _():
            for m in range(micro):
                for q in range(parts):
                    if q < per:
                        @pl.when(me != q)
                        def _():
                            top_copy(m, q).wait_send()
                    else:
                        top_copy(m, q).wait_send()

        @pl.when(section < pipes - 1)
        def _():
            wo_copy.wait_send()
            for m in range(micro):
                for copy in hid_copies[m]:
                    copy.wait_send()
    else:
        for m in range(micro):
            for copy in hid_copies[m]:
                copy.wait_send()
    for m in range(micro):
        for copy in dp_copies[m]:
            copy.wait_send()

        @pl.when(section > 0)
        def _():
            for copy in g_copies[m]:
                copy.wait_send()


def shards(acts, w_in, w_out, top_grad):
    pipes = lax.axis_size("pipe")
    parts = lax.axis_size("tensor")
    pair = lax.axis_size("dp") == 2 and parts % 2 == 0
    saved = acts[0]
    micro, rows, width = saved.shape
    if pair:
        w_in_now, w_out_now = w_in[0], w_out[0]
    else:
        w_in_now = lax.all_gather(w_in[0], "dp", axis=1, tiled=True)
        w_out_now = lax.all_gather(w_out[0], "dp", axis=0, tiled=True)
    own = w_in_now.shape[1]
    per = parts // 2 if pair else parts
    quarter = own // per
    chunks = 4
    others = parts - 1
    bf, f32 = jnp.bfloat16, jnp.float32
    dma = pltpu.SemaphoreType.DMA
    vmem = pl.BlockSpec(memory_space=pltpu.VMEM)
    across = []
    if pair:
        across = [
            pltpu.VMEM((width, own), bf),
            pltpu.VMEM((own, width), bf),
            pltpu.VMEM((micro, rows, width), bf),
            pltpu.VMEM((micro, rows, width), bf),
            pltpu.VMEM((micro, per, rows, quarter), bf),
            pltpu.VMEM((per, micro * rows, quarter), bf),
            dma((4,)), dma((4,)),
            dma((micro,)), dma((micro,)), dma((micro,)), dma((micro,)),
            pltpu.VMEM((micro, parts, rows, quarter), f32),
            dma((micro, parts)), dma((micro, parts)),
        ]
    back, grad_in, grad_out = pl.pallas_call(
        functools.partial(chain, pipes, parts, pair, chunks),
        out_shape=(
            jax.ShapeDtypeStruct((micro, rows, width), bf),
            jax.ShapeDtypeStruct((width, own), bf),
            jax.ShapeDtypeStruct((own, width), bf),
        ),
        in_specs=[vmem] * 4,
        out_specs=(vmem,) * 3,
        scratch_shapes=[
            pltpu.VMEM((micro, rows, width), bf),
            pltpu.VMEM((parts, micro * rows, quarter), f32),
            pltpu.VMEM((others, micro * rows, quarter), f32),
            pltpu.VMEM((parts, micro * rows, quarter), bf),
            pltpu.VMEM((micro, parts, rows, quarter), f32),
            pltpu.VMEM((micro, others, rows, quarter), f32),
            pltpu.VMEM((micro, parts, rows, quarter), bf),
            pltpu.VMEM((micro * rows, quarter), f32),
            dma((others,)), dma((others,)), dma((others,)), dma((others,)),
            dma((micro, others)), dma((micro, others)),
            dma((micro, others)), dma((micro, others)),
            dma((micro, chunks)), dma((micro, chunks)),
            *across,
        ],
        compiler_params=pltpu.CompilerParams(
            collective_id=0, has_side_effects=True, vmem_limit_bytes=48 * 1024 * 1024
        ),
    )(saved, w_in_now, w_out_now, top_grad)
    if not pair:
        grad_in = lax.psum_scatter(grad_in, "dp", scatter_dimension=1, tiled=True)
        grad_out = lax.psum_scatter(grad_out, "dp", scatter_dimension=0, tiled=True)
    return back[None], grad_in[None], grad_out[None]


def solution(mesh):
    placed = (
        P("pipe", None, "dp", "tensor"),
        P("pipe", "tensor", "dp"),
        P("pipe", "dp", "tensor"),
        P(None, "dp", "tensor"),
    )
    return jax.shard_map(
        shards,
        mesh=mesh,
        in_specs=placed,
        out_specs=(
            P("pipe", None, "dp", "tensor"),
            P("pipe", "tensor", "dp"),
            P("pipe", "dp", "tensor"),
        ),
        check_vma=False,
    )
```
